512 devices in a mesh: tm: 128 (over z, y, core), chan: 4 (over x).
Axes of the slice: x: 4, y: 4, z: 16, core: 2. Of those that a mesh axis runs over, the one named last changes fastest.
Arguments:
- markov: float32 [16384, 256, 4], P('tm', 'chan'), may hold values from -6 to 6
- sketch: float32 [16384, 4, 64], P('tm'), may hold values from -0.0234375 to 0.0234375
Outputs:
- basis: float32 [16384, 256, 64], P('tm', 'chan')
- factor: float32 [64, 64], replicated
The draws below stay inside these ranges and needn't reach their ends.
All inputs are finite; a program needn't handle non-finite values.
Results may differ from the reference program's by a relative error of at most 0.000098.
Values sent between devices are 32-bit elements; how exact they have to be, the bound alone decides.
A program may use at most 128 MiB of HBM per device.

```python
import jax
import jax.numpy as jnp
from jax import lax

CHANNELS = 256
INPUTS = 4
COLUMNS = 64
TIME = 16384


def shard_levels(stream_key, extent, cuts, smallest, high):
    loudness = 1.0
    for axis_at, parts in cuts:
        draws = jax.random.uniform(jax.random.fold_in(jax.random.fold_in(stream_key, 6), axis_at), (parts,), jnp.float32, smallest / len(cuts), high / len(cuts))
        loudness = loudness * jnp.repeat(jnp.exp(draws), extent[axis_at] // parts).reshape((-1,) + (1,) * (len(extent) - 1 - axis_at))
    return loudness


def noise(own_key, dims, scale, reach, pieces=(), held_as=jnp.bfloat16):
    loudness = shard_levels(own_key, dims, pieces, -0.22, 0.18) if pieces else 1.0
    array = jax.random.normal(own_key, dims, jnp.float32) * scale * loudness
    return jnp.minimum(jnp.maximum(array, -reach), reach).astype(held_as)


def setup_inputs(seed: int = 0) -> dict:
    streams_of = jax.random.split(jax.random.key(seed), 3)
    markov = noise(streams_of[0], (TIME, CHANNELS, INPUTS), 1.0, 6.0, ((0, 128), (1, 4)), jnp.float32)
    sketch = noise(streams_of[1], (TIME, INPUTS, COLUMNS), (TIME * INPUTS) ** -0.5, 0.0234375, ((0, 128),), jnp.float32)
    return dict(markov=markov, sketch=sketch)


chan_block = 16

def reference(markov, sketch):
    whole_len = markov.shape[0]
    sketch_hat = jnp.conj(jnp.fft.fft(sketch, axis=0))
    stacked = markov.reshape(whole_len, CHANNELS // chan_block, chan_block, INPUTS).transpose(1, 0, 2, 3)

    def one_block(piece):
        spectrum = jnp.fft.fft(piece, axis=0)
        mixed = jnp.einsum('tpm,tmr->tpr', spectrum, sketch_hat)
        return jnp.real(jnp.fft.ifft(mixed, axis=0)).astype(jnp.float32)
    signal = lax.map(one_block, stacked)
    signal = signal.transpose(1, 0, 2, 3).reshape(whole_len, CHANNELS, COLUMNS)
    gram = jnp.einsum('tpr,tps->rs', signal, signal, precision=lax.Precision.HIGHEST) / (whole_len * CHANNELS)
    lower_factor = jnp.linalg.cholesky(gram)
    identity_m = jnp.eye(COLUMNS, dtype=jnp.float32)
    inverse_t = jax.scipy.linalg.solve_triangular(lower_factor, identity_m, lower=True).T
    basis = jnp.einsum('tpr,rs->tps', signal, inverse_t, precision=lax.Precision.HIGHEST)
    return (basis, lower_factor.T)
```

```python
import functools

import jax
import jax.numpy as jnp
import ml_dtypes
import numpy as np
from jax import lax
from jax.experimental import pallas as pl
from jax.experimental.pallas import tpu as pltpu
from jax.sharding import PartitionSpec as P

HIGH = lax.Precision.HIGH
HIGHEST = lax.Precision.HIGHEST
MESH = pl.DeviceIdType.MESH
GROUP = 8


def reduce_kernel(depth, width, gram_ref, out_ref, first, mine, along, total, own, got,
                  send1, recv1, send2, recv2, send3, recv3):
    tm = lax.axis_index("tm")
    ch = lax.axis_index("chan")
    plane = tm // GROUP
    seat = tm - plane * GROUP

    def at(zi, si, ci):
        return (zi * GROUP + si, ci)

    barrier = pltpu.get_barrier_semaphore()
    for k in range(1, GROUP):
        pl.semaphore_signal(barrier, inc=1, device_id=at(plane, lax.rem(seat + k, GROUP), ch), device_id_type=MESH)
    for k in range(1, depth):
        pl.semaphore_signal(barrier, inc=1, device_id=at(lax.rem(plane + k, depth), seat, ch), device_id_type=MESH)
    for c in range(1, width):
        for k in range(GROUP):
            pl.semaphore_signal(barrier, inc=1, device_id=at(plane, lax.rem(seat + k, GROUP), lax.rem(ch + c, width)), device_id_type=MESH)
    pl.semaphore_wait(barrier, GROUP - 1 + depth - 1 + (width - 1) * GROUP)

    copies = []
    for k in range(1, GROUP):
        to = lax.rem(seat + k, GROUP)
        copies.append(pltpu.make_async_remote_copy(
            src_ref=gram_ref.at[to], dst_ref=first.at[k - 1],
            send_sem=send1.at[k - 1], recv_sem=recv1.at[k - 1],
            device_id=at(plane, to, ch), device_id_type=MESH))
    for copy in copies:
        copy.start()
    value = gram_ref[seat]
    for copy in copies:
        copy.wait()
    for k in range(1, GROUP):
        value = value + first[k - 1]
    mine[...] = value
    copies = []
    for k in range(1, depth):
        copies.append(pltpu.make_async_remote_copy(
            src_ref=mine, dst_ref=along.at[k - 1],
            send_sem=send2.at[k - 1], recv_sem=recv2.at[k - 1],
            device_id=at(lax.rem(plane + k, depth), seat, ch), device_id_type=MESH))
    for copy in copies:
        copy.start()
    for copy in copies:
        copy.wait()
    total[...] = jnp.zeros_like(total)
    for z in range(depth):
        back = lax.rem(plane - z + depth, depth)

        @pl.when(back == 0)
        def _():
            total[...] += mine[...]

        @pl.when(back != 0)
        def _():
            total[...] += along[lax.max(back - 1, 0)]
    own[...] = total[...]
    copies = []
    for c in range(width):
        for k in range(GROUP):
            if c == 0 and k == 0:
                continue
            slot = c * GROUP + k
            copies.append(pltpu.make_async_remote_copy(
                src_ref=own, dst_ref=got.at[slot],
                send_sem=send3.at[slot], recv_sem=recv3.at[slot],
                device_id=at(plane, lax.rem(seat + k, GROUP), lax.rem(ch + c, width)), device_id_type=MESH))
    for copy in copies:
        copy.start()
    got[0] = own[...]
    for copy in copies:
        copy.wait()
    for s in range(GROUP):
        k = lax.rem(seat - s + GROUP, GROUP)
        acc = jnp.zeros_like(own)
        for c in range(width):
            acc = acc + got[lax.rem(ch - c + width, width) * GROUP + k]
        out_ref[s] = acc


def total_gram(part, depth, width):
    tile = (8, 64)
    return pl.pallas_call(
        functools.partial(reduce_kernel, depth, width),
        out_shape=jax.ShapeDtypeStruct((GROUP,) + tile, jnp.float32),
        in_specs=[pl.BlockSpec(memory_space=pltpu.VMEM)],
        out_specs=pl.BlockSpec(memory_space=pltpu.VMEM),
        scratch_shapes=[
            pltpu.VMEM((GROUP - 1,) + tile, jnp.float32),
            pltpu.VMEM(tile, jnp.float32),
            pltpu.VMEM((depth - 1,) + tile, jnp.float32),
            pltpu.VMEM(tile, jnp.float32),
            pltpu.VMEM(tile, jnp.float32),
            pltpu.VMEM((width * GROUP,) + tile, jnp.float32),
            pltpu.SemaphoreType.DMA((GROUP - 1,)),
            pltpu.SemaphoreType.DMA((GROUP - 1,)),
            pltpu.SemaphoreType.DMA((depth - 1,)),
            pltpu.SemaphoreType.DMA((depth - 1,)),
            pltpu.SemaphoreType.DMA((width * GROUP,)),
            pltpu.SemaphoreType.DMA((width * GROUP,)),
        ],
        compiler_params=pltpu.CompilerParams(collective_id=1, has_side_effects=True),
    )(part.reshape((GROUP,) + tile)).reshape(64, 64)


def split(x):
    high = x.astype(jnp.bfloat16)
    return high, (x - high.astype(jnp.float32)).astype(jnp.bfloat16)


def outer(a, b):
    return lax.dot_general(a, b, (((1,), (1,)), ((), ())), preferred_element_type=jnp.float32)


def inner(a, b):
    return jnp.dot(a, b, preferred_element_type=jnp.float32)


def waves(block):
    n = np.arange(block)
    f = np.arange(block)
    angle = (2.0 * np.pi / (4 * block)) * ((n[None, :] * (2 * f[:, None] + 1)) % (4 * block))
    forward = np.stack([np.cos(angle), -np.sin(angle)], axis=1).reshape(2 * block, block)
    backward = np.concatenate([np.cos(angle).T, -np.sin(angle).T], axis=1) / block

    def pieces(x):
        high = x.astype(ml_dtypes.bfloat16)
        return high, (x - high.astype(np.float64)).astype(ml_dtypes.bfloat16)

    fh, fl = pieces(forward)
    bh, bl = pieces(backward)
    return (jnp.asarray(np.concatenate([fh, fh], axis=1)), jnp.asarray(fl),
            jnp.asarray(bh), jnp.asarray(bl))


def spectrum_kernel(block, shards, rows, x_ref, s_ref, fhh_ref, fl_ref, bh_ref, bl_ref,
                    sig_ref, gram_ref, hx, hs, mix):
    step = pl.program_id(0)
    last = pl.num_programs(0) - 1
    me = lax.axis_index("tm")

    def transform(slab, dst):
        src = slab.reshape(shards * rows, block)

        @pl.loop(0, rows // 2)
        def _(pair):
            p = pair * 2
            x = jnp.concatenate([
                src[pl.ds(p, shards, stride=rows), :],
                src[pl.ds(p + 1, shards, stride=rows), :]], axis=0)
            high, low = split(x)
            both = jnp.concatenate([high, low], axis=1)
            out = outer(fhh_ref[...], both) + outer(fl_ref[...], high)
            dst[pl.ds(p, 2 * block, stride=rows), :] = out[:, :shards]
            dst[pl.ds(p + 1, 2 * block, stride=rows), :] = out[:, shards:]

    transform(x_ref, hx)
    transform(s_ref, hs)

    def product(f):
        at = pl.multiple_of(f * 2 * rows, 2 * rows)
        h = hx[pl.ds(at, 2 * rows), :]
        t_re = hs[pl.ds(at, rows), :]
        t_im = hs[pl.ds(at + rows, rows), :]
        sign = (1 - 2 * lax.rem(f, 2)).astype(jnp.float32)
        here = pltpu.roll(jnp.concatenate([t_re, t_im], axis=0), me, 1)
        past = pltpu.roll(jnp.concatenate([-t_im, t_re], axis=0), me + 1, 1)
        t = here + sign * past
        hh, hl = split(h)
        th, tl = split(t)
        return outer(jnp.concatenate([hh, hl], axis=1), jnp.concatenate([th, th], axis=1)) + outer(hh, tl)

    @pl.when(step == 0)
    def _():
        @pl.loop(0, block)
        def _(f):
            mix[pl.ds(f, 2 * rows, stride=block), :] = product(f)

    @pl.when(step != 0)
    def _():
        @pl.loop(0, block)
        def _(f):
            mix[pl.ds(f, 2 * rows, stride=block), :] += product(f)

    @pl.when(step == last)
    def _():
        gram_ref[...] = jnp.zeros_like(gram_ref)

        @pl.loop(0, rows // 2)
        def _(pair):
            def parts(p):
                zero = mix[pl.ds(pl.multiple_of(p * block, block), block), :]
                one = mix[pl.ds(pl.multiple_of((rows + p) * block, block), block), :]
                return zero + pltpu.roll(one, rows, 1), one - pltpu.roll(zero, rows, 1)

            re0, im0 = parts(pair * 2)
            re1, im1 = parts(pair * 2 + 1)
            lane = lax.broadcasted_iota(jnp.int32, re0.shape, 1)
            re = jnp.where(lane < rows, re0, pltpu.roll(re1, rows, 1))
            im = jnp.where(lane < rows, im0, pltpu.roll(im1, rows, 1))
            high, low = split(jnp.concatenate([re, im], axis=0))
            out = inner(bh_ref[...], high) + inner(bh_ref[...], low) + inner(bl_ref[...], high)
            sig = out.T
            sig_ref[pl.ds(pl.multiple_of(pair * 2 * rows, 2 * rows), 2 * rows), :] = sig
            gram_ref[...] += lax.dot_general(
                sig, sig, (((1,), (1,)), ((), ())), precision=HIGHEST,
                preferred_element_type=jnp.float32)


def image(all_m, all_s, block, shards, rows, inputs):
    tables = waves(block)
    assert block == shards == 2 * rows
    whole = lambda x: pl.BlockSpec(x.shape, lambda m: (0, 0), pipeline_mode=pl.Buffered(1))
    slab = pl.BlockSpec((shards, None, rows, block), lambda m: (0, m, 0, 0))
    return pl.pallas_call(
        functools.partial(spectrum_kernel, block, shards, rows),
        grid=(inputs,),
        out_shape=(jax.ShapeDtypeStruct((rows * rows, block), jnp.float32),
                   jax.ShapeDtypeStruct((2 * rows, 2 * rows), jnp.float32)),
        in_specs=[slab, slab] + [whole(x) for x in tables],
        out_specs=(pl.BlockSpec((rows * rows, block), lambda m: (0, 0)),
                   pl.BlockSpec((2 * rows, 2 * rows), lambda m: (0, 0))),
        scratch_shapes=[pltpu.VMEM((2 * block * rows, shards), jnp.float32),
                        pltpu.VMEM((2 * block * rows, shards), jnp.float32),
                        pltpu.VMEM((2 * rows * block, 2 * rows), jnp.float32)],
        compiler_params=pltpu.CompilerParams(
            dimension_semantics=("arbitrary",), vmem_limit_bytes=60 * 2**20),
    )(all_m, all_s, *tables)


def body(markov, sketch):
    block, channels, inputs = markov.shape
    columns = sketch.shape[2]
    shards = lax.axis_size("tm")
    width = lax.axis_size("chan")
    row_total = block * shards * channels * width

    own_m = markov.transpose(2, 1, 0)
    own_s = sketch.transpose(1, 2, 0)
    all_m = lax.all_gather(own_m, "tm", axis=0, tiled=False)
    all_s = lax.all_gather(own_s, "tm", axis=0, tiled=False)
    sig, gram_two = image(all_m, all_s, block, shards, channels, inputs)
    signal = sig.reshape(channels, columns, block)
    gram_part = gram_two[:columns, :columns] + gram_two[columns:, columns:]
    gram = total_gram(gram_part, shards // GROUP, width)
    lower = jnp.linalg.cholesky(gram / row_total)
    eye = jnp.eye(columns, dtype=jnp.float32)
    inverse_t = jax.scipy.linalg.solve_triangular(lower, eye, lower=True).T
    basis = jnp.einsum("prb,rs->bps", signal, inverse_t, precision=HIGH)
    return basis, lower.T


def solution(mesh):
    return jax.shard_map(
        body,
        mesh=mesh,
        in_specs=(P("tm", "chan", None), P("tm", None, None)),
        out_specs=(P("tm", "chan", None), P()),
        check_vma=False,
    )
```

```python
import functools

import jax
import jax.numpy as jnp
import ml_dtypes
import numpy as np
from jax import lax
from jax.experimental import pallas as pl
from jax.experimental.pallas import tpu as pltpu
from jax.sharding import PartitionSpec as P

HIGH = lax.Precision.HIGH
HIGHEST = lax.Precision.HIGHEST
MESH = pl.DeviceIdType.MESH
EIGHT = 8
PIECES = 1
UNROLL = 8
GROUP = 8


def reduce_kernel(depth, width, gram_ref, out_ref, first, mine, along, total, own, got,
                  send1, recv1, send2, recv2, send3, recv3):
    tm = lax.axis_index("tm")
    ch = lax.axis_index("chan")
    plane = tm // GROUP
    seat = tm - plane * GROUP

    def at(zi, si, ci):
        return (zi * GROUP + si, ci)

    barrier = pltpu.get_barrier_semaphore()
    for k in range(1, GROUP):
        pl.semaphore_signal(barrier, inc=1, device_id=at(plane, lax.rem(seat + k, GROUP), ch), device_id_type=MESH)
    for k in range(1, depth):
        pl.semaphore_signal(barrier, inc=1, device_id=at(lax.rem(plane + k, depth), seat, ch), device_id_type=MESH)
    for c in range(1, width):
        for k in range(GROUP):
            pl.semaphore_signal(barrier, inc=1, device_id=at(plane, lax.rem(seat + k, GROUP), lax.rem(ch + c, width)), device_id_type=MESH)
    pl.semaphore_wait(barrier, GROUP - 1 + depth - 1 + (width - 1) * GROUP)

    copies = []
    for k in range(1, GROUP):
        to = lax.rem(seat + k, GROUP)
        copies.append(pltpu.make_async_remote_copy(
            src_ref=gram_ref.at[to], dst_ref=first.at[k - 1],
            send_sem=send1.at[k - 1], recv_sem=recv1.at[k - 1],
            device_id=at(plane, to, ch), device_id_type=MESH))
    for copy in copies:
        copy.start()
    value = gram_ref[seat]
    for copy in copies:
        copy.wait()
    for k in range(1, GROUP):
        value = value + first[k - 1]
    mine[...] = value
    copies = []
    for k in range(1, depth):
        copies.append(pltpu.make_async_remote_copy(
            src_ref=mine, dst_ref=along.at[k - 1],
            send_sem=send2.at[k - 1], recv_sem=recv2.at[k - 1],
            device_id=at(lax.rem(plane + k, depth), seat, ch), device_id_type=MESH))
    for copy in copies:
        copy.start()
    for copy in copies:
        copy.wait()
    total[...] = jnp.zeros_like(total)
    for z in range(depth):
        back = lax.rem(plane - z + depth, depth)

        @pl.when(back == 0)
        def _():
            total[...] += mine[...]

        @pl.when(back != 0)
        def _():
            total[...] += along[lax.max(back - 1, 0)]
    own[...] = total[...]
    copies = []
    for c in range(width):
        for k in range(GROUP):
            if c == 0 and k == 0:
                continue
            slot = c * GROUP + k
            copies.append(pltpu.make_async_remote_copy(
                src_ref=own, dst_ref=got.at[slot],
                send_sem=send3.at[slot], recv_sem=recv3.at[slot],
                device_id=at(plane, lax.rem(seat + k, GROUP), lax.rem(ch + c, width)), device_id_type=MESH))
    for copy in copies:
        copy.start()
    got[0] = own[...]
    for copy in copies:
        copy.wait()
    for s in range(GROUP):
        k = lax.rem(seat - s + GROUP, GROUP)
        acc = jnp.zeros_like(own)
        for c in range(width):
            acc = acc + got[lax.rem(ch - c + width, width) * GROUP + k]
        out_ref[s] = acc


def total_gram(part, depth, width):
    tile = (8, 64)
    return pl.pallas_call(
        functools.partial(reduce_kernel, depth, width),
        out_shape=jax.ShapeDtypeStruct((GROUP,) + tile, jnp.float32),
        in_specs=[pl.BlockSpec(memory_space=pltpu.VMEM)],
        out_specs=pl.BlockSpec(memory_space=pltpu.VMEM),
        scratch_shapes=[
            pltpu.VMEM((GROUP - 1,) + tile, jnp.float32),
            pltpu.VMEM(tile, jnp.float32),
            pltpu.VMEM((depth - 1,) + tile, jnp.float32),
            pltpu.VMEM(tile, jnp.float32),
            pltpu.VMEM(tile, jnp.float32),
            pltpu.VMEM((width * GROUP,) + tile, jnp.float32),
            pltpu.SemaphoreType.DMA((GROUP - 1,)),
            pltpu.SemaphoreType.DMA((GROUP - 1,)),
            pltpu.SemaphoreType.DMA((depth - 1,)),
            pltpu.SemaphoreType.DMA((depth - 1,)),
            pltpu.SemaphoreType.DMA((width * GROUP,)),
            pltpu.SemaphoreType.DMA((width * GROUP,)),
        ],
        compiler_params=pltpu.CompilerParams(collective_id=1, has_side_effects=True),
    )(part.reshape((GROUP,) + tile)).reshape(64, 64)


def split(x):
    high = x.astype(jnp.bfloat16)
    return high, (x - high.astype(jnp.float32)).astype(jnp.bfloat16)


def outer(a, b):
    return lax.dot_general(a, b, (((1,), (1,)), ((), ())), preferred_element_type=jnp.float32)


def inner(a, b):
    return jnp.dot(a, b, preferred_element_type=jnp.float32)


def waves(block):
    n = np.arange(block)
    f = np.arange(block)
    angle = (2.0 * np.pi / (4 * block)) * ((n[None, :] * (2 * f[:, None] + 1)) % (4 * block))
    forward = np.stack([np.cos(angle), -np.sin(angle)], axis=1).reshape(2 * block, block)
    backward = np.concatenate([np.cos(angle).T, -np.sin(angle).T], axis=1) / block

    def pieces(x):
        high = x.astype(ml_dtypes.bfloat16)
        return high, (x - high.astype(np.float64)).astype(ml_dtypes.bfloat16)

    fh, fl = pieces(forward)
    bh, bl = pieces(backward)
    return (jnp.asarray(np.concatenate([fh, fh], axis=1)), jnp.asarray(fl),
            jnp.asarray(bh), jnp.asarray(bl))


def spectrum_kernel(block, shards, rows, x_ref, s_ref, fhh_ref, fl_ref, bh_ref, bl_ref,
                    sig_ref, gram_ref, hx, hs, mix):
    step = pl.program_id(0)
    last = pl.num_programs(0) - 1
    me = lax.axis_index("tm")

    def transform(src, dst):
        planes = dst.reshape(2 * block, rows, shards)

        @pl.loop(0, rows // EIGHT)
        def _(part):
            at = pl.multiple_of(part * EIGHT, EIGHT)
            x = jnp.swapaxes(src[:, pl.ds(at, EIGHT), :], 0, 1)
            high, low = split(x.reshape(EIGHT * shards, block))
            both = jnp.concatenate([high, low], axis=1)
            for piece in range(PIECES):
                span = slice(piece * 2 * block // PIECES, (piece + 1) * 2 * block // PIECES)
                out = outer(fhh_ref[span], both) + outer(fl_ref[span], high)
                out = jnp.stack([out[:, k * shards:(k + 1) * shards] for k in range(EIGHT)])
                planes[span, pl.ds(at, EIGHT), :] = jnp.swapaxes(out, 0, 1)

    transform(x_ref, hx)
    transform(s_ref, hs)

    def product(f, parity):
        at = pl.multiple_of(f * 2 * rows, 2 * rows)
        h = hx[pl.ds(at, 2 * rows), :]
        t = hs[pl.ds(at, 2 * rows), :]
        past = pltpu.roll(t, me + 1, 1)
        past = jnp.concatenate([-past[rows:], past[:rows]], axis=0)
        here = pltpu.roll(t, me, 1)
        t = here + past if parity == 0 else here - past
        hh, hl = split(h)
        th, tl = split(t)
        return outer(jnp.concatenate([hh, hl], axis=1), jnp.concatenate([th, th], axis=1)) + outer(hh, tl)

    def products(first):
        @pl.loop(0, block // UNROLL)
        def _(turn):
            for k in range(UNROLL):
                f = turn * UNROLL + k
                span = pl.ds(pl.multiple_of(f * 2 * rows, 2 * rows), 2 * rows)
                value = product(f, k % 2)
                mix[span, :] = value if first else mix[span, :] + value

    pl.when(step == 0)(lambda: products(True))
    pl.when(step != 0)(lambda: products(False))

    @pl.when(step == last)
    def _():
        gram_ref[...] = jnp.zeros_like(gram_ref)
        planes = mix.reshape(block, 2 * rows, 2 * rows)
        lane = lax.broadcasted_iota(jnp.int32, (block, 2 * rows), 1)

        @pl.loop(0, rows // EIGHT)
        def _(part):
            at = pl.multiple_of(part * EIGHT, EIGHT)
            zeros = jnp.swapaxes(planes[:, pl.ds(at, EIGHT), :], 0, 1)
            ones = jnp.swapaxes(planes[:, pl.ds(rows + at, EIGHT), :], 0, 1)

            def parts(k):
                return zeros[k] + pltpu.roll(ones[k], rows, 1), ones[k] - pltpu.roll(zeros[k], rows, 1)

            for k in range(0, EIGHT, 2):
                re0, im0 = parts(k)
                re1, im1 = parts(k + 1)
                re = jnp.where(lane < rows, re0, pltpu.roll(re1, rows, 1))
                im = jnp.where(lane < rows, im0, pltpu.roll(im1, rows, 1))
                high, low = split(jnp.concatenate([re, im], axis=0))
                out = inner(bh_ref[...], high) + inner(bh_ref[...], low) + inner(bl_ref[...], high)
                sig = out.T
                sig_ref[pl.ds(pl.multiple_of((at + k) * rows, 2 * rows), 2 * rows), :] = sig
                gram_ref[...] += lax.dot_general(
                    sig, sig, (((1,), (1,)), ((), ())), precision=HIGHEST,
                    preferred_element_type=jnp.float32)


def image(gathered, block, shards, rows, inputs):
    tables = waves(block)
    assert block == shards == 2 * rows
    whole = lambda x: pl.BlockSpec(x.shape, lambda m: (0, 0), pipeline_mode=pl.Buffered(1))
    slab = lambda first: pl.BlockSpec((shards, None, rows, block), lambda m: (0, first + m, 0, 0))
    return pl.pallas_call(
        functools.partial(spectrum_kernel, block, shards, rows),
        grid=(inputs,),
        out_shape=(jax.ShapeDtypeStruct((rows * rows, block), jnp.float32),
                   jax.ShapeDtypeStruct((2 * rows, 2 * rows), jnp.float32)),
        in_specs=[slab(0), slab(inputs)] + [whole(x) for x in tables],
        out_specs=(pl.BlockSpec((rows * rows, block), lambda m: (0, 0)),
                   pl.BlockSpec((2 * rows, 2 * rows), lambda m: (0, 0))),
        scratch_shapes=[pltpu.VMEM((2 * block * rows, shards), jnp.float32),
                        pltpu.VMEM((2 * block * rows, shards), jnp.float32),
                        pltpu.VMEM((2 * rows * block, 2 * rows), jnp.float32)],
        compiler_params=pltpu.CompilerParams(
            dimension_semantics=("arbitrary",), vmem_limit_bytes=60 * 2**20),
    )(gathered, gathered, *tables)


def body(markov, sketch):
    block, channels, inputs = markov.shape
    columns = sketch.shape[2]
    shards = lax.axis_size("tm")
    width = lax.axis_size("chan")
    row_total = block * shards * channels * width

    own_m = markov.transpose(2, 1, 0)
    own_s = sketch.transpose(1, 2, 0)
    gathered = lax.all_gather(jnp.concatenate([own_m, own_s]), "tm", axis=0, tiled=False)
    sig, gram_two = image(gathered, block, shards, channels, inputs)
    signal = sig.reshape(channels, columns, block)
    gram_part = gram_two[:columns, :columns] + gram_two[columns:, columns:]
    gram = total_gram(gram_part, shards // GROUP, width)
    lower = jnp.linalg.cholesky(gram / row_total)
    eye = jnp.eye(columns, dtype=jnp.float32)
    inverse_t = jax.scipy.linalg.solve_triangular(lower, eye, lower=True).T
    basis = jnp.einsum("prb,rs->bps", signal, inverse_t, precision=HIGH)
    return basis, lower.T


def solution(mesh):
    return jax.shard_map(
        body,
        mesh=mesh,
        in_specs=(P("tm", "chan", None), P("tm", None, None)),
        out_specs=(P("tm", "chan", None), P()),
        check_vma=False,
    )
```

```python
import functools

import jax
import jax.numpy as jnp
import ml_dtypes
import numpy as np
from jax import lax
from jax.experimental import pallas as pl
from jax.experimental.pallas import tpu as pltpu
from jax.sharding import PartitionSpec as P

HIGH = lax.Precision.HIGH
HIGHEST = lax.Precision.HIGHEST
MESH = pl.DeviceIdType.MESH
EIGHT = 8
PIECES = 1
UNROLL = 8
SPLIT = 5
RING = 4
GROUP = 8


def reduce_kernel(depth, width, gram_ref, out_ref, first, mine, along, total, own, got,
                  send1, recv1, send2, recv2, send3, recv3):
    tm = lax.axis_index("tm")
    ch = lax.axis_index("chan")
    plane = tm // GROUP
    seat = tm - plane * GROUP

    def at(zi, si, ci):
        return (zi * GROUP + si, ci)

    barrier = pltpu.get_barrier_semaphore()
    for k in range(1, GROUP):
        pl.semaphore_signal(barrier, inc=1, device_id=at(plane, lax.rem(seat + k, GROUP), ch), device_id_type=MESH)
    for k in range(1, depth):
        pl.semaphore_signal(barrier, inc=1, device_id=at(lax.rem(plane + k, depth), seat, ch), device_id_type=MESH)
    for c in range(1, width):
        for k in range(GROUP):
            pl.semaphore_signal(barrier, inc=1, device_id=at(plane, lax.rem(seat + k, GROUP), lax.rem(ch + c, width)), device_id_type=MESH)
    pl.semaphore_wait(barrier, GROUP - 1 + depth - 1 + (width - 1) * GROUP)

    copies = []
    for k in range(1, GROUP):
        to = lax.rem(seat + k, GROUP)
        copies.append(pltpu.make_async_remote_copy(
            src_ref=gram_ref.at[to], dst_ref=first.at[k - 1],
            send_sem=send1.at[k - 1], recv_sem=recv1.at[k - 1],
            device_id=at(plane, to, ch), device_id_type=MESH))
    for copy in copies:
        copy.start()
    value = gram_ref[seat]
    for copy in copies:
        copy.wait()
    for k in range(1, GROUP):
        value = value + first[k - 1]
    mine[...] = value
    copies = []
    for k in range(1, depth):
        copies.append(pltpu.make_async_remote_copy(
            src_ref=mine, dst_ref=along.at[k - 1],
            send_sem=send2.at[k - 1], recv_sem=recv2.at[k - 1],
            device_id=at(lax.rem(plane + k, depth), seat, ch), device_id_type=MESH))
    for copy in copies:
        copy.start()
    for copy in copies:
        copy.wait()
    total[...] = jnp.zeros_like(total)
    for z in range(depth):
        back = lax.rem(plane - z + depth, depth)

        @pl.when(back == 0)
        def _():
            total[...] += mine[...]

        @pl.when(back != 0)
        def _():
            total[...] += along[lax.max(back - 1, 0)]
    own[...] = total[...]
    copies = []
    for c in range(width):
        for k in range(GROUP):
            if c == 0 and k == 0:
                continue
            slot = c * GROUP + k
            copies.append(pltpu.make_async_remote_copy(
                src_ref=own, dst_ref=got.at[slot],
                send_sem=send3.at[slot], recv_sem=recv3.at[slot],
                device_id=at(plane, lax.rem(seat + k, GROUP), lax.rem(ch + c, width)), device_id_type=MESH))
    for copy in copies:
        copy.start()
    got[0] = own[...]
    for copy in copies:
        copy.wait()
    for s in range(GROUP):
        k = lax.rem(seat - s + GROUP, GROUP)
        acc = jnp.zeros_like(own)
        for c in range(width):
            acc = acc + got[lax.rem(ch - c + width, width) * GROUP + k]
        out_ref[s] = acc


def total_gram(part, depth, width):
    tile = (8, 64)
    return pl.pallas_call(
        functools.partial(reduce_kernel, depth, width),
        out_shape=jax.ShapeDtypeStruct((GROUP,) + tile, jnp.float32),
        in_specs=[pl.BlockSpec(memory_space=pltpu.VMEM)],
        out_specs=pl.BlockSpec(memory_space=pltpu.VMEM),
        scratch_shapes=[
            pltpu.VMEM((GROUP - 1,) + tile, jnp.float32),
            pltpu.VMEM(tile, jnp.float32),
            pltpu.VMEM((depth - 1,) + tile, jnp.float32),
            pltpu.VMEM(tile, jnp.float32),
            pltpu.VMEM(tile, jnp.float32),
            pltpu.VMEM((width * GROUP,) + tile, jnp.float32),
            pltpu.SemaphoreType.DMA((GROUP - 1,)),
            pltpu.SemaphoreType.DMA((GROUP - 1,)),
            pltpu.SemaphoreType.DMA((depth - 1,)),
            pltpu.SemaphoreType.DMA((depth - 1,)),
            pltpu.SemaphoreType.DMA((width * GROUP,)),
            pltpu.SemaphoreType.DMA((width * GROUP,)),
        ],
        compiler_params=pltpu.CompilerParams(collective_id=1, has_side_effects=True),
    )(part.reshape((GROUP,) + tile)).reshape(64, 64)


def gather_kernel(depth, x_ref, out_ref, own_sem, send_sems, recv_sems):
    tm = lax.axis_index("tm")
    ch = lax.axis_index("chan")
    z = tm // GROUP
    y = (tm - z * GROUP) // 2
    core = tm - z * GROUP - y * 2
    half = x_ref.shape[1] // 2
    lower, upper = pl.ds(0, half), pl.ds(half, half)
    head, tail = pl.ds(0, SPLIT), pl.ds(SPLIT, x_ref.shape[0] - SPLIT)
    turn = lambda k: lax.rem(z + k + depth, depth)
    side = lambda k: lax.rem(y + k + RING, RING)
    device = lambda zi, yi, ci: ((zi * RING + yi) * 2 + ci, ch)
    up, down = device(turn(1), y, core), device(turn(-1), y, core)
    right, left = device(z, side(1), core), device(z, side(-1), core)
    other = device(z, y, 1 - core)

    barrier = pltpu.get_barrier_semaphore()
    for peer in (up, down, right, left, other):
        pl.semaphore_signal(barrier, inc=1, device_id=peer, device_id_type=MESH)
    pl.semaphore_wait(barrier, 5)

    copies = []

    def send(part, to, source=None):
        slot = len(copies)
        copy = pltpu.make_async_remote_copy(
            src_ref=part if source is None else source, dst_ref=part,
            send_sem=send_sems.at[slot], recv_sem=recv_sems.at[slot],
            device_id=to, device_id_type=MESH)
        copy.start()
        copies.append(copy)
        return copy

    def received(*some):
        for copy in some:
            copy.wait_recv()

    def along_y(zi, source=None):
        part = out_ref.at[zi, y, core, head]
        return zi, send(part, right, source), send(part, left, source)

    def across_y(zi, one, two):
        received(one, two)
        return (zi, send(out_ref.at[zi, side(-1), core, head, lower], right),
                send(out_ref.at[zi, side(1), core, head, upper], left))

    last = []

    def to_core(zi, rows):
        last.append(send(out_ref.at[zi, :, core, rows], other))

    own = pltpu.make_async_copy(x_ref, out_ref.at[z, y, core], own_sem)
    own.start()
    first = x_ref.at[head]
    second = x_ref.at[tail]
    row = out_ref.at[z, y, core, tail]
    b_right, b_left = send(row, right, second), send(row, left, second)
    a_up = send(out_ref.at[z, y, core, head], up, first)
    a_down = send(out_ref.at[z, y, core, head], down, first)
    received(b_right, b_left)
    b_right = send(out_ref.at[z, side(-1), core, tail, lower], right)
    b_left = send(out_ref.at[z, side(1), core, tail, upper], left)
    direct = [along_y(z, first)]
    own.wait()
    received(b_right, b_left)
    b_up = send(out_ref.at[z, :, core, tail], up)
    b_down = send(out_ref.at[z, :, core, tail], down)
    to_core(z, tail)
    crossing = []
    middle = depth // 2
    for step in range(1, middle + 1):
        received(a_up, a_down)
        zu, zd = turn(-step), turn(step)
        if step < middle - 1:
            a_up = send(out_ref.at[zu, y, core, head], up)
            a_down = send(out_ref.at[zd, y, core, head], down)
        elif step == middle - 1:
            a_up = send(out_ref.at[zu, y, core, head, lower], up)
            a_down = send(out_ref.at[zd, y, core, head, upper], down)
        for block in crossing:
            received(*block[1:])
            to_core(block[0], head)
        crossing = [across_y(*block) for block in direct]
        direct = [along_y(zu)] + ([along_y(zd)] if step < middle else [])
        received(b_up, b_down)
        if step < middle - 1:
            b_up = send(out_ref.at[zu, :, core, tail], up)
            b_down = send(out_ref.at[zd, :, core, tail], down)
        elif step == middle - 1:
            b_up = send(out_ref.at[zu, :, core, tail, lower], up)
            b_down = send(out_ref.at[zd, :, core, tail, upper], down)
        to_core(zu, tail)
        if step < middle:
            to_core(zd, tail)
    final = [across_y(*block) for block in direct]
    for block in crossing + final:
        received(*block[1:])
        to_core(block[0], head)
    received(*last)
    for copy in copies:
        copy.wait_send()


def gather(own, shards):
    depth = shards // GROUP
    count = 15 * depth
    return pl.pallas_call(
        functools.partial(gather_kernel, depth),
        out_shape=jax.ShapeDtypeStruct((depth, RING, 2) + own.shape, jnp.float32),
        in_specs=[pl.BlockSpec(memory_space=pltpu.VMEM)],
        out_specs=pl.BlockSpec(memory_space=pl.ANY),
        scratch_shapes=[pltpu.SemaphoreType.DMA,
                        pltpu.SemaphoreType.DMA((count,)),
                        pltpu.SemaphoreType.DMA((count,))],
        compiler_params=pltpu.CompilerParams(collective_id=2, has_side_effects=True),
    )(own).reshape((shards,) + own.shape)


def split(x):
    high = x.astype(jnp.bfloat16)
    return high, (x - high.astype(jnp.float32)).astype(jnp.bfloat16)


def outer(a, b):
    return lax.dot_general(a, b, (((1,), (1,)), ((), ())), preferred_element_type=jnp.float32)


def inner(a, b):
    return jnp.dot(a, b, preferred_element_type=jnp.float32)


def waves(block):
    n = np.arange(block)
    f = np.arange(block)
    angle = (2.0 * np.pi / (4 * block)) * ((n[None, :] * (2 * f[:, None] + 1)) % (4 * block))
    forward = np.stack([np.cos(angle), -np.sin(angle)], axis=1).reshape(2 * block, block)
    backward = np.concatenate([np.cos(angle).T, -np.sin(angle).T], axis=1) / block

    def pieces(x):
        high = x.astype(ml_dtypes.bfloat16)
        return high, (x - high.astype(np.float64)).astype(ml_dtypes.bfloat16)

    fh, fl = pieces(forward)
    bh, bl = pieces(backward)
    return (jnp.asarray(np.concatenate([fh, fh], axis=1)), jnp.asarray(fl),
            jnp.asarray(bh), jnp.asarray(bl))


def spectrum_kernel(block, shards, rows, x_ref, s_ref, fhh_ref, fl_ref, bh_ref, bl_ref,
                    sig_ref, gram_ref, hx, hs, mix):
    step = pl.program_id(0)
    last = pl.num_programs(0) - 1
    me = lax.axis_index("tm")

    def transform(src, dst):
        planes = dst.reshape(2 * block, rows, shards)

        @pl.loop(0, rows // EIGHT)
        def _(part):
            at = pl.multiple_of(part * EIGHT, EIGHT)
            x = jnp.swapaxes(src[:, pl.ds(at, EIGHT), :], 0, 1)
            high, low = split(x.reshape(EIGHT * shards, block))
            both = jnp.concatenate([high, low], axis=1)
            for piece in range(PIECES):
                span = slice(piece * 2 * block // PIECES, (piece + 1) * 2 * block // PIECES)
                out = outer(fhh_ref[span], both) + outer(fl_ref[span], high)
                out = jnp.stack([out[:, k * shards:(k + 1) * shards] for k in range(EIGHT)])
                planes[span, pl.ds(at, EIGHT), :] = jnp.swapaxes(out, 0, 1)

    transform(x_ref, hx)
    transform(s_ref, hs)

    def product(f, parity):
        at = pl.multiple_of(f * 2 * rows, 2 * rows)
        h = hx[pl.ds(at, 2 * rows), :]
        t = hs[pl.ds(at, 2 * rows), :]
        past = pltpu.roll(t, me + 1, 1)
        past = jnp.concatenate([-past[rows:], past[:rows]], axis=0)
        here = pltpu.roll(t, me, 1)
        t = here + past if parity == 0 else here - past
        hh, hl = split(h)
        th, tl = split(t)
        return outer(jnp.concatenate([hh, hl], axis=1), jnp.concatenate([th, th], axis=1)) + outer(hh, tl)

    def products(first):
        @pl.loop(0, block // UNROLL)
        def _(turn):
            for k in range(UNROLL):
                f = turn * UNROLL + k
                span = pl.ds(pl.multiple_of(f * 2 * rows, 2 * rows), 2 * rows)
                value = product(f, k % 2)
                mix[span, :] = value if first else mix[span, :] + value

    pl.when(step == 0)(lambda: products(True))
    pl.when(step != 0)(lambda: products(False))

    @pl.when(step == last)
    def _():
        gram_ref[...] = jnp.zeros_like(gram_ref)
        planes = mix.reshape(block, 2 * rows, 2 * rows)
        lane = lax.broadcasted_iota(jnp.int32, (block, 2 * rows), 1)

        @pl.loop(0, rows // EIGHT)
        def _(part):
            at = pl.multiple_of(part * EIGHT, EIGHT)
            zeros = jnp.swapaxes(planes[:, pl.ds(at, EIGHT), :], 0, 1)
            ones = jnp.swapaxes(planes[:, pl.ds(rows + at, EIGHT), :], 0, 1)

            def parts(k):
                return zeros[k] + pltpu.roll(ones[k], rows, 1), ones[k] - pltpu.roll(zeros[k], rows, 1)

            for k in range(0, EIGHT, 2):
                re0, im0 = parts(k)
                re1, im1 = parts(k + 1)
                re = jnp.where(lane < rows, re0, pltpu.roll(re1, rows, 1))
                im = jnp.where(lane < rows, im0, pltpu.roll(im1, rows, 1))
                high, low = split(jnp.concatenate([re, im], axis=0))
                out = inner(bh_ref[...], high) + inner(bh_ref[...], low) + inner(bl_ref[...], high)
                sig = out.T
                sig_ref[pl.ds(pl.multiple_of((at + k) * rows, 2 * rows), 2 * rows), :] = sig
                gram_ref[...] += lax.dot_general(
                    sig, sig, (((1,), (1,)), ((), ())), precision=HIGHEST,
                    preferred_element_type=jnp.float32)


def image(gathered, block, shards, rows, inputs):
    tables = waves(block)
    assert block == shards == 2 * rows
    whole = lambda x: pl.BlockSpec(x.shape, lambda m: (0, 0), pipeline_mode=pl.Buffered(1))
    slab = lambda first: pl.BlockSpec((shards, None, rows, block), lambda m: (0, first + m, 0, 0))
    return pl.pallas_call(
        functools.partial(spectrum_kernel, block, shards, rows),
        grid=(inputs,),
        out_shape=(jax.ShapeDtypeStruct((rows * rows, block), jnp.float32),
                   jax.ShapeDtypeStruct((2 * rows, 2 * rows), jnp.float32)),
        in_specs=[slab(0), slab(inputs)] + [whole(x) for x in tables],
        out_specs=(pl.BlockSpec((rows * rows, block), lambda m: (0, 0)),
                   pl.BlockSpec((2 * rows, 2 * rows), lambda m: (0, 0))),
        scratch_shapes=[pltpu.VMEM((2 * block * rows, shards), jnp.float32),
                        pltpu.VMEM((2 * block * rows, shards), jnp.float32),
                        pltpu.VMEM((2 * rows * block, 2 * rows), jnp.float32)],
        compiler_params=pltpu.CompilerParams(
            dimension_semantics=("arbitrary",), vmem_limit_bytes=60 * 2**20),
    )(gathered, gathered, *tables)


def body(markov, sketch):
    block, channels, inputs = markov.shape
    columns = sketch.shape[2]
    shards = lax.axis_size("tm")
    width = lax.axis_size("chan")
    row_total = block * shards * channels * width

    own_m = markov.transpose(2, 1, 0)
    own_s = sketch.transpose(1, 2, 0)
    gathered = gather(jnp.concatenate([own_m, own_s]), shards)
    sig, gram_two = image(gathered, block, shards, channels, inputs)
    signal = sig.reshape(channels, columns, block)
    gram_part = gram_two[:columns, :columns] + gram_two[columns:, columns:]
    gram = total_gram(gram_part, shards // GROUP, width)
    lower = jnp.linalg.cholesky(gram / row_total)
    eye = jnp.eye(columns, dtype=jnp.float32)
    inverse_t = jax.scipy.linalg.solve_triangular(lower, eye, lower=True).T
    basis = jnp.einsum("prb,rs->bps", signal, inverse_t, precision=HIGH)
    return basis, lower.T


def solution(mesh):
    return jax.shard_map(
        body,
        mesh=mesh,
        in_specs=(P("tm", "chan", None), P("tm", None, None)),
        out_specs=(P("tm", "chan", None), P()),
        check_vma=False,
    )
```
